32 devices in a mesh: gx: 2 (over core), gy: 4 (over y, x), gz: 4 (over z).
Axes of the slice: x: 2, y: 2, z: 4, core: 2. Of those that a mesh axis runs over, the one named last changes fastest.
Arguments:
- heights: float32 [8192, 1024], P(('gy', 'gz'), 'gx'), may hold values from -6 to 6
- scene_ids: int32 [8192, 1024], P(('gy', 'gz'), 'gx'), may hold values from 0 to 15, as said below
- scene_offset: float32 [16], replicated, may hold values from -4 to 4
- scene_weight: float32 [16], replicated, may hold values from 0.2 to 5
- band_gain: float32 [6], replicated, may hold values from 0.3 to 1.5
Outputs:
- blended: float32 [8192, 1024], P(('gy', 'gz'), 'gx')
The draws below stay inside these ranges and needn't reach their ends.
Inputs may be any that keep to these rules, and one draw needn't show every extreme that they name: `scene_ids`: scene index of each cell.
All inputs are finite; a program needn't handle non-finite values.
Results may differ from the reference program's by a relative error of at most 0.00002.
Values sent between devices are 32-bit elements; how exact they have to be, the bound alone decides.
A program may use at most 128 MiB of HBM per device.

```python
import math
import jax
import jax.numpy as jnp

SCENES = 16
LEVELS = 6
NR = 8192
NC = 1024


def draw_scene_ids(key, part):
    key_grid = jax.random.fold_in(key, 11)
    key_jitter = jax.random.fold_in(key, 23)
    grid = jax.random.randint(key_grid, (NR // 48 + 2, NC // 48 + 2), 0, SCENES).astype(jnp.int32)
    grid = grid.at[0, 0].set(SCENES - 1).at[0, 1].set(0)
    jitter = jax.random.randint(key_jitter, (NR,), 0, 16).astype(jnp.int32)
    row_cell = (jnp.arange(NR, dtype=jnp.int32) // 48)[:, None]
    col_cell = (jnp.arange(NC, dtype=jnp.int32)[None, :] + jitter[:, None]) // 48
    return grid[row_cell, col_cell].astype(jnp.int32)


def shard_levels(stream_key, extent, split, least, top_value):
    def one(dim, shards_of):
        steps = jax.random.uniform(jax.random.fold_in(jax.random.fold_in(stream_key, 6), dim), (shards_of,), jnp.float32, least / len(split), top_value / len(split))
        return jnp.repeat(jnp.exp(steps), extent[dim] // shards_of).reshape((-1,) + (1,) * (len(extent) - dim - 1))

    factor_of = one(*split[0])
    for cut in split[1:]:
        factor_of = factor_of * one(*cut)
    return factor_of


def gaussian(stream_key, dims, scale, bound, cuts=(), kind=jnp.bfloat16):
    values = scale * jax.random.normal(stream_key, dims, jnp.float32)
    if cuts:
        values = values * shard_levels(stream_key, dims, cuts, -0.22, 0.18)
    return jnp.clip(values, -bound, bound).astype(kind)


def setup_inputs(seed: int = 0) -> dict:
    key_of = jax.random.split(jax.random.key(seed), 6)
    return {
        "heights": gaussian(key_of[0], (NR, NC), 1.0, 6.0, ((0, 16), (1, 2)), jnp.float32),
        "scene_ids": draw_scene_ids(jax.random.fold_in(key_of[5], 71), 0),
        "scene_offset": jnp.clip(jax.random.uniform(key_of[2], (SCENES,), jnp.float32, -4.0, 4.0), -4.0, 4.0),
        "scene_weight": jnp.clip(jnp.exp(jax.random.uniform(key_of[3], (SCENES,), jnp.float32, math.log(0.2), math.log(5.0))), 0.2, 5.0),
        "band_gain": jnp.clip(jnp.exp(jax.random.uniform(key_of[4], (LEVELS,), jnp.float32, math.log(0.3), math.log(1.5))), 0.3, 1.5),
    }


KERN = (0.0625, 0.25, 0.375, 0.25, 0.0625)


def lookup(scene_ids, table):
    acc = jnp.zeros(scene_ids.shape, jnp.float32)
    for scene in range(SCENES):
        acc = acc + jnp.where(scene_ids == scene, table[scene], jnp.float32(0.0))
    return acc


def reduce_padded(padded):
    rows_out = padded.shape[-2] - 4
    cols_out = padded.shape[-1] - 4
    rows = KERN[0] * padded[..., 0:rows_out:2, :]
    for tap in range(1, 5):
        rows = rows + KERN[tap] * padded[..., tap:tap + rows_out:2, :]
    result = KERN[0] * rows[..., 0:cols_out:2]
    for tap in range(1, 5):
        result = result + KERN[tap] * rows[..., tap:tap + cols_out:2]
    return result


def expand_padded(padded):
    count = padded.shape[-2] - 2
    even = (padded[..., 0:count, :] + 6.0 * padded[..., 1:count + 1, :] + padded[..., 2:count + 2, :]) * 0.125
    odd = (padded[..., 1:count + 1, :] + padded[..., 2:count + 2, :]) * 0.5
    rows = jnp.stack([even, odd], axis=-2)
    rows = rows.reshape(rows.shape[:-3] + (2 * count, rows.shape[-1]))
    width = rows.shape[-1] - 2
    even = (rows[..., 0:width] + 6.0 * rows[..., 1:width + 1] + rows[..., 2:width + 2]) * 0.125
    odd = (rows[..., 1:width + 1] + rows[..., 2:width + 2]) * 0.5
    result = jnp.stack([even, odd], axis=-1)
    return result.reshape(result.shape[:-2] + (2 * width,))


def reference(heights, scene_ids, scene_offset, scene_weight, band_gain):
    weight = lookup(scene_ids, scene_weight)
    offset = lookup(scene_ids, scene_offset)
    numer = weight * (heights + offset)
    denom = weight
    ratios = [numer / denom]
    for level in range(LEVELS):
        numer = reduce_padded(jnp.pad(numer, 2))
        denom = reduce_padded(jnp.pad(denom, 2))
        ratios.append(numer / denom)
    top_mean = jnp.sum(numer) / jnp.sum(denom)
    collapsed = jnp.zeros_like(ratios[LEVELS]) + top_mean
    for level in range(LEVELS - 1, -1, -1):
        band = ratios[level] - expand_padded(jnp.pad(ratios[level + 1], 1))
        collapsed = band_gain[level] * band + expand_padded(jnp.pad(collapsed, 1))
    return collapsed
```

```python
import functools

import jax
import jax.numpy as jnp
import numpy as np
from jax import lax
from jax.experimental import pallas as pl
from jax.experimental.pallas import tpu as pltpu
from jax.sharding import PartitionSpec as P

F32, BF16 = jnp.float32, jnp.bfloat16
FAR = 1 << 20
HALO = 16
SIDE = 128
EDGE3 = 24
TAPS = (0.375, 0.25, 0.0625)
LEVELS = 6


def reach(count):
    weights = np.ones(count >> LEVELS, np.float64)
    for _ in range(LEVELS):
        fine = np.zeros(2 * weights.size + 4, np.float64)
        for tap, value in zip(range(-2, 3), (0.0625, 0.25, 0.375, 0.25, 0.0625)):
            fine[2 + tap : 2 + tap + 2 * weights.size : 2] += value * weights
        weights = fine[2:-2]
    return weights.astype(np.float32)


def split(x):
    high = x.astype(BF16)
    return high, (x - high.astype(F32)).astype(BF16)


def right(x, c):
    high, low = split(x)
    return jnp.dot(high, c, preferred_element_type=F32) + jnp.dot(
        low, c, preferred_element_type=F32
    )


def left(r, x):
    high, low = split(x)
    return jnp.dot(r, high, preferred_element_type=F32) + jnp.dot(
        r, low, preferred_element_type=F32
    )


def band(distance, scale):
    far = jnp.abs(distance)
    value = jnp.where(far == 2, TAPS[2] * scale, 0.0)
    value = jnp.where(far == 1, TAPS[1] * scale, value)
    value = jnp.where(far == 0, TAPS[0] * scale, value)
    return value.astype(F32).astype(BF16)


def kernel(
    sizes, off_ref, wgt_ref, gain_ref, h_ref, s_ref, u_ref, v_ref, out_ref,
    h_buf, s_buf, u_buf, v_buf, nh, nl, dh, dl, b3, part, slots,
    own_sem, send0, recv0, send3, recv3, psend, precv,
):
    nr, nc, nx, ny, nz, rows_total, cols_total = sizes
    cx, cy, cz = lax.axis_index("gx"), lax.axis_index("gy"), lax.axis_index("gz")
    row = cy * nz + cz
    blocks = ny * nz
    w3 = nc // 8
    t3 = nr // 8

    def device(drow, dcol):
        target = row + drow
        return {"gx": cx + dcol, "gy": target // nz, "gz": target % nz}

    has = {-1: (row > 0, cx > 0), 0: None, 1: (row < blocks - 1, cx < nx - 1)}

    def there(drow, dcol):
        ok = None
        if drow:
            ok = has[drow][0]
        if dcol:
            ok = has[dcol][1] if ok is None else jnp.logical_and(ok, has[dcol][1])
        return ok

    dirs = [(a, b) for a in (-1, 0, 1) for b in (-1, 0, 1) if a or b]
    axes = (("gx", nx, cx), ("gz", nz, cz), ("gy", ny, cy))

    own = []
    for i, (src, dst) in enumerate(
        (
            (h_ref, h_buf.at[pl.ds(0, nr), pl.ds(0, nc)]),
            (s_ref, s_buf.at[pl.ds(0, nr), pl.ds(0, nc)]),
            (u_ref.at[row], u_buf),
            (v_ref.at[cx], v_buf),
        )
    ):
        copy = pltpu.make_async_copy(src, dst, own_sem.at[i])
        copy.start()
        own.append(copy)

    barrier = pltpu.get_barrier_semaphore()
    for d in dirs:
        @pl.when(there(*d))
        def _():
            pl.semaphore_signal(barrier, inc=1, device_id=device(*d))
    for name, count, me in axes:
        for step in range(1, count):
            pl.semaphore_signal(barrier, inc=1, device_id={name: (me + step) % count})

    def iota(n, dim):
        return lax.broadcasted_iota(jnp.int32, (n, 1) if dim == 0 else (1, n), dim)

    def fold(index, first, total, level):
        base = first >> level
        ok = jnp.logical_and(index + base >= 0, index + base < (total >> level))
        return jnp.where(ok, index, FAR)

    row0, col0 = row * nr, cx * nc
    r1, r2 = nr // 2 + 16, nr // 4 + 16
    c1, c2 = nc // 2 + 128, nc // 4 + 128
    r3, r4, r5, r6 = t3 + 2 * EDGE3, nr // 16 + 32, nr // 32 + 16, nr // 64 + 8

    def rows_at(level, dim):
        if level == 0:
            p = iota(nr + 2 * HALO, dim)
            return jnp.where(p < nr, p, jnp.where(p < nr + HALO, p - nr - HALO, p - HALO))
        count, shift = ((r1, 8), (r2, 8), (r3, EDGE3), (r4, 16), (r5, 8), (r6, 4))[level - 1]
        return iota(count, dim) - shift

    def cols_at(level, dim):
        if level == 0:
            p = iota(nc + 2 * SIDE, dim)
            return jnp.where(p < nc, p, jnp.where(p < nc + SIDE, p - nc - SIDE, p - SIDE))
        if level < 3:
            return iota((c1, c2)[level - 1], dim) - 8
        if level == 3:
            p = iota(6 * w3, dim)
            return (p // (2 * w3) - 1) * w3 + p % w3
        return iota(2 * w3, dim) % w3 - (16, 8, 4)[level - 4]

    def kind(count, dim):
        return (iota(count, dim) // w3) % 2

    def reduce_rows(level):
        out = fold(rows_at(level + 1, 0), row0, rows_total, level + 1)
        return band(rows_at(level, 1) - 2 * out, 1.0)

    def reduce_cols(level):
        out = fold(cols_at(level + 1, 1), col0, cols_total, level + 1)
        distance = cols_at(level, 0) - 2 * out
        if level >= 3:
            same = kind(distance.shape[0], 0) == kind(distance.shape[1], 1)
            distance = jnp.where(same, distance, FAR)
        return band(distance, 1.0)

    def expand_rows(level):
        out = iota(nr, 0) if level == 0 else rows_at(level, 0)
        return band(2 * rows_at(level + 1, 1) - out, 2.0)

    def expand_cols(level):
        out = iota(nc, 1) if level == 0 else cols_at(level, 1)
        return band(2 * cols_at(level + 1, 0) - out, 2.0)

    near = sum(there(*d).astype(jnp.int32) for d in dirs)
    pl.semaphore_wait(barrier, near + (nx + ny + nz - 3))

    def rim(i, a, d):
        drow, dcol = d
        src, dst = ((h_ref, h_buf), (s_ref, s_buf))[a]
        rs = {-1: (0, nr + HALO, HALO), 0: (0, 0, nr), 1: (nr - HALO, nr, HALO)}[drow]
        cs = {-1: (0, nc + SIDE, SIDE), 0: (0, 0, nc), 1: (nc - SIDE, nc, SIDE)}[dcol]
        return pltpu.make_async_remote_copy(
            src_ref=src.at[pl.ds(rs[0], rs[2]), pl.ds(cs[0], cs[2])],
            dst_ref=dst.at[pl.ds(rs[1], rs[2]), pl.ds(cs[1], cs[2])],
            send_sem=send0.at[2 * i + a],
            recv_sem=recv0.at[2 * i + a],
            device_id=device(*d),
        )

    for i, d in enumerate(dirs):
        @pl.when(there(*d))
        def _():
            for a in range(2):
                rim(i, a, d).start()

    def lookup(masks, table):
        values = [table[i] for i in range(table.shape[0])]
        for mask in masks:
            values = [
                jnp.where(mask, values[i + 1], values[i]) for i in range(0, len(values), 2)
            ]
        return values[0]

    bits = (off_ref.shape[0] - 1).bit_length()

    def level0(rows, cols, valid):
        ids = s_buf[rows, cols]
        masks = [(ids & (1 << bit)) != 0 for bit in range(bits)]
        weight = lookup(masks, wgt_ref)
        moved = h_buf[rows, cols] + lookup(masks, off_ref)
        numer = weight * moved
        if valid is not None:
            weight = jnp.where(valid, weight, 0.0)
            numer = jnp.where(valid, numer, 0.0)
        nh[rows, cols], nl[rows, cols] = split(numer)
        dh[rows, cols], dl[rows, cols] = split(weight)
        return moved

    for copy in own:
        copy.wait()

    step = 32

    def own_rows(i, carry):
        rows = pl.ds(pl.multiple_of(i * step, step), step)
        out_ref[rows, :] = level0(rows, pl.ds(0, nc), None)
        return carry

    lax.fori_loop(0, nr // step, own_rows, 0)

    reduce0 = reduce_rows(0)
    u_high, u_low = split(u_buf[...])
    pick = iota(16, 0)
    u_rows = jnp.where(
        pick == 0, u_high.astype(F32), jnp.where(pick == 1, u_low.astype(F32), 0.0)
    ).astype(BF16)
    top = jnp.concatenate([reduce0[:, :nr], u_rows], axis=0)
    rim0 = reduce0[:, nr:]

    def dot(a, b):
        return jnp.dot(a, b, preferred_element_type=F32)

    tn = dot(top, nh[pl.ds(0, nr), pl.ds(0, nc)]) + dot(top, nl[pl.ds(0, nr), pl.ds(0, nc)])
    td = dot(top, dh[pl.ds(0, nr), pl.ds(0, nc)]) + dot(top, dl[pl.ds(0, nr), pl.ds(0, nc)])
    v_row = v_buf[...]
    sum_n = jnp.sum(tn[r1:, :] * v_row)
    sum_d = jnp.sum(td[r1:, :] * v_row)

    tile_row = lax.broadcasted_iota(jnp.int32, (8, 128), 0)
    part[0] = jnp.where(tile_row == 0, sum_n, jnp.where(tile_row == 1, sum_d, 0.0))

    starts = (0, nx - 1, nx + nz - 2)

    def phase(k):
        name, count, me = axes[k]
        return [
            pltpu.make_async_remote_copy(
                src_ref=part.at[k],
                dst_ref=slots.at[starts[k] + s - 1],
                send_sem=psend.at[starts[k] + s - 1],
                recv_sem=precv.at[starts[k] + s - 1],
                device_id={name: (me + s) % count},
            )
            for s in range(1, count)
        ]

    def finish(k):
        total = part[k]
        for s, copy in enumerate(phase(k)):
            copy.wait()
            total = total + slots[starts[k] + s]
        return total

    for copy in phase(0):
        copy.start()

    for i, d in enumerate(dirs):
        @pl.when(there(*d))
        def _():
            for a in range(2):
                rim(i, a, d).wait_send()

        @pl.when(there(-d[0], -d[1]))
        def _():
            for a in range(2):
                rim(i, a, d).wait_recv()

    def yes(flag):
        return flag.astype(jnp.int32)

    up, down = yes(row > 0), yes(row < blocks - 1)
    west, east = yes(cx > 0), yes(cx < nx - 1)

    def row_ok(p):
        return jnp.where(p < nr, 1, jnp.where(p < nr + HALO, up, down))

    level0(pl.ds(nr, 2 * HALO), pl.ds(0, nc), jnp.broadcast_to(row_ok(iota(2 * HALO, 0) + nr), (2 * HALO, nc)) > 0)
    side_ok = jnp.where(iota(2 * SIDE, 1) < SIDE, west, east)

    def side_rows(i, carry):
        rows = pl.ds(pl.multiple_of(i * step, step), step)
        level0(rows, pl.ds(nc, 2 * SIDE), (row_ok(iota(step, 0) + i * step) * side_ok) > 0)
        return carry

    lax.fori_loop(0, (nr + 2 * HALO) // step, side_rows, 0)

    rim_r, side_c = pl.ds(nr, 2 * HALO), pl.ds(nc, 2 * SIDE)
    cols0 = reduce_cols(0)

    def level1(t_own, high, low):
        t_own = t_own[:r1, :] + dot(rim0, high[rim_r, pl.ds(0, nc)]) + dot(rim0, low[rim_r, pl.ds(0, nc)])
        t_side = dot(reduce0, high[:, side_c]) + dot(reduce0, low[:, side_c])
        return right(t_own, cols0[:nc]) + right(t_side, cols0[nc:])

    n1, d1 = level1(tn, nh, nl), level1(td, dh, dl)

    part[1] = finish(0)
    for copy in phase(1):
        copy.start()

    rows1, cols1 = reduce_rows(1), reduce_cols(1)
    n2, d2 = left(rows1, right(n1, cols1)), left(rows1, right(d1, cols1))

    own_out = iota(2 * w3, 1)
    in2 = cols_at(2, 0)
    pick_n = band(jnp.where(own_out < w3, in2 - 2 * own_out, FAR), 1.0)
    pick_d = band(jnp.where(own_out < w3, FAR, in2 - 2 * (own_out - w3)), 1.0)
    own_rows3 = band(rows_at(2, 1) - 2 * iota(t3, 0), 1.0)
    both = right(n2, pick_n) + right(d2, pick_d)
    b3[1, pl.ds(EDGE3, t3), :] = left(own_rows3, both)

    def rim3(i, d):
        drow, dcol = d
        rs = {
            -1: (EDGE3, EDGE3 + t3, EDGE3),
            0: (EDGE3, EDGE3, t3),
            1: (t3, 0, EDGE3),
        }[drow]
        return pltpu.make_async_remote_copy(
            src_ref=b3.at[1, pl.ds(rs[0], rs[2]), :],
            dst_ref=b3.at[1 - dcol, pl.ds(rs[1], rs[2]), :],
            send_sem=send3.at[i],
            recv_sem=recv3.at[i],
            device_id=device(*d),
        )

    for i, d in enumerate(dirs):
        @pl.when(there(*d))
        def _():
            rim3(i, d).start()

    q1 = jnp.where(d1 > 0, n1 / d1, 0.0)
    q2 = jnp.where(d2 > 0, n2 / d2, 0.0)
    part[2] = finish(1)
    for copy in phase(2):
        copy.start()

    rows_ = [None, None, None] + [reduce_rows(level) for level in (3, 4, 5)]
    cols_ = [None, None, None] + [reduce_cols(level) for level in (3, 4, 5)]
    up_rows = [expand_rows(level) for level in range(6)]
    up_cols = [expand_cols(level) for level in range(6)]

    for i, d in enumerate(dirs):
        @pl.when(there(*d))
        def _():
            rim3(i, d).wait_send()

        @pl.when(there(-d[0], -d[1]))
        def _():
            rim3(i, d).wait_recv()

    p3 = iota(r3, 0)
    ok3 = jnp.where(p3 < EDGE3, up, jnp.where(p3 < EDGE3 + t3, 1, down))
    lane = iota(2 * w3, 1)

    def ratio(packed):
        weights = pltpu.roll(packed, w3, axis=1)
        ok = jnp.logical_and(weights > 0, jnp.broadcast_to(lane, packed.shape) < w3)
        return jnp.where(ok, packed / weights, 0.0), ok

    pieces = []
    for block, flag in ((0, west), (1, None), (2, east)):
        ok = ok3 if flag is None else ok3 * flag
        piece = b3[block]
        pieces.append(jnp.where(jnp.broadcast_to(ok, piece.shape) > 0, piece, 0.0))
    packed = jnp.concatenate(pieces, axis=1)
    q3 = [ratio(piece) for piece in pieces]
    q3, ok_3 = [q for q, _ in q3], [jnp.where(ok, 1.0, 0.0) for _, ok in q3]
    q3, ok_3 = jnp.concatenate(q3, axis=1), jnp.concatenate(ok_3, axis=1) > 0

    v4 = left(rows_[3], right(packed, cols_[3]))
    v5 = left(rows_[4], right(v4, cols_[4]))
    v6 = left(rows_[5], right(v5, cols_[5]))
    q4, ok_4 = ratio(v4)
    q5, ok_5 = ratio(v5)
    q6, ok_6 = ratio(v6)

    total = finish(2)
    top_sum = jnp.sum(jnp.where(tile_row == 0, total, 0.0), axis=0, keepdims=True)
    top_weight = jnp.sum(jnp.where(tile_row == 1, total, 0.0), axis=0, keepdims=True)
    top_mean = (top_sum / top_weight)[:, :1]

    z = jnp.where(ok_6, top_mean - gain_ref[5] * q6, 0.0)
    levels = ((5, q5, ok_5), (4, q4, ok_4), (3, q3, ok_3), (2, q2, d2 > 0), (1, q1, d1 > 0))
    for level, q, ok in levels:
        grown = left(up_rows[level], right(z, up_cols[level]))
        z = jnp.where(ok, grown + (gain_ref[level] - gain_ref[level - 1]) * q, 0.0)
    wide = right(z, up_cols[0])
    out_ref[...] = gain_ref[0] * out_ref[...] + left(up_rows[0], wide)


def local(mesh_shape, heights, scene_ids, scene_offset, scene_weight, band_gain):
    nx, ny, nz = mesh_shape
    nr, nc = heights.shape
    rows_total, cols_total = nr * ny * nz, nc * nx
    u = jnp.asarray(reach(rows_total).reshape(ny * nz, 1, nr))
    v = jnp.asarray(reach(cols_total).reshape(nx, 1, nc))
    sizes = (nr, nc, nx, ny, nz, rows_total, cols_total)
    ext = (nr + 2 * HALO, nc + 2 * SIDE)
    peers = nx + ny + nz - 3
    smem = pl.BlockSpec(memory_space=pltpu.SMEM)
    hbm = pl.BlockSpec(memory_space=pl.ANY)
    return pl.pallas_call(
        functools.partial(kernel, sizes),
        out_shape=jax.ShapeDtypeStruct((nr, nc), F32),
        in_specs=[smem, smem, smem, hbm, hbm, hbm, hbm],
        out_specs=pl.BlockSpec(memory_space=pltpu.VMEM),
        scratch_shapes=[
            pltpu.VMEM(ext, F32),
            pltpu.VMEM(ext, jnp.int32),
            pltpu.VMEM((1, nr), F32),
            pltpu.VMEM((1, nc), F32),
            pltpu.VMEM(ext, BF16),
            pltpu.VMEM(ext, BF16),
            pltpu.VMEM(ext, BF16),
            pltpu.VMEM(ext, BF16),
            pltpu.VMEM((3, nr // 8 + 2 * EDGE3, nc // 4), F32),
            pltpu.VMEM((3, 8, 128), F32),
            pltpu.VMEM((peers, 8, 128), F32),
            pltpu.SemaphoreType.DMA((4,)),
            pltpu.SemaphoreType.DMA((16,)),
            pltpu.SemaphoreType.DMA((16,)),
            pltpu.SemaphoreType.DMA((8,)),
            pltpu.SemaphoreType.DMA((8,)),
            pltpu.SemaphoreType.DMA((peers,)),
            pltpu.SemaphoreType.DMA((peers,)),
        ],
        compiler_params=pltpu.CompilerParams(collective_id=0, has_side_effects=True),
    )(scene_offset, scene_weight, band_gain, heights, scene_ids, u, v)


def solution(mesh):
    placed = (P(("gy", "gz"), "gx"), P(("gy", "gz"), "gx"), P(), P(), P())
    shape = tuple(mesh.shape[name] for name in ("gx", "gy", "gz"))
    return jax.shard_map(
        functools.partial(local, shape), mesh=mesh, in_specs=placed,
        out_specs=P(("gy", "gz"), "gx"), check_vma=False,
    )
```

```python
import functools

import jax
import jax.numpy as jnp
import numpy as np
from jax import lax
from jax.experimental import pallas as pl
from jax.experimental.pallas import tpu as pltpu
from jax.sharding import PartitionSpec as P

F32, BF16 = jnp.float32, jnp.bfloat16
FAR = 1 << 20
HALO = 16
SIDE = 128
EDGE3 = 24
TAPS = (0.375, 0.25, 0.0625)
LEVELS = 6


def reach(count):
    weights = np.ones(count >> LEVELS, np.float64)
    for _ in range(LEVELS):
        fine = np.zeros(2 * weights.size + 4, np.float64)
        for tap, value in zip(range(-2, 3), (0.0625, 0.25, 0.375, 0.25, 0.0625)):
            fine[2 + tap : 2 + tap + 2 * weights.size : 2] += value * weights
        weights = fine[2:-2]
    return weights.astype(np.float32)


def split(x):
    high = x.astype(BF16)
    return high, (x - high.astype(F32)).astype(BF16)


def right(x, c):
    high, low = split(x)
    return jnp.dot(high, c, preferred_element_type=F32) + jnp.dot(
        low, c, preferred_element_type=F32
    )


def left(r, x):
    high, low = split(x)
    return jnp.dot(r, high, preferred_element_type=F32) + jnp.dot(
        r, low, preferred_element_type=F32
    )


def band(distance, scale):
    far = jnp.abs(distance)
    value = jnp.where(far == 2, TAPS[2] * scale, 0.0)
    value = jnp.where(far == 1, TAPS[1] * scale, value)
    value = jnp.where(far == 0, TAPS[0] * scale, value)
    return value.astype(F32).astype(BF16)


def kernel(
    sizes, off_ref, wgt_ref, gain_ref, h_ref, s_ref, u_ref, v_ref, z1_ref, q0_ref,
    q0, h_buf, s_buf, u_buf, v_buf, nh, nl, dh, dl, b3, part, slots,
    own_sem, send0, recv0, send3, recv3, psend, precv,
):
    nr, nc, nx, ny, nz, rows_total, cols_total = sizes
    cx, cy, cz = lax.axis_index("gx"), lax.axis_index("gy"), lax.axis_index("gz")
    row = cy * nz + cz
    blocks = ny * nz
    w3 = nc // 8
    t3 = nr // 8

    def device(drow, dcol):
        target = row + drow
        return {"gx": cx + dcol, "gy": target // nz, "gz": target % nz}

    has = {-1: (row > 0, cx > 0), 0: None, 1: (row < blocks - 1, cx < nx - 1)}

    def there(drow, dcol):
        ok = None
        if drow:
            ok = has[drow][0]
        if dcol:
            ok = has[dcol][1] if ok is None else jnp.logical_and(ok, has[dcol][1])
        return ok

    dirs = [(a, b) for a in (-1, 0, 1) for b in (-1, 0, 1) if a or b]
    axes = (("gx", nx, cx), ("gz", nz, cz), ("gy", ny, cy))

    own = []
    for i, (src, dst) in enumerate(
        (
            (h_ref, h_buf.at[pl.ds(0, nr), pl.ds(0, nc)]),
            (s_ref, s_buf.at[pl.ds(0, nr), pl.ds(0, nc)]),
            (u_ref.at[row], u_buf),
            (v_ref.at[cx], v_buf),
        )
    ):
        copy = pltpu.make_async_copy(src, dst, own_sem.at[i])
        copy.start()
        own.append(copy)

    barrier = pltpu.get_barrier_semaphore()
    for d in dirs:
        @pl.when(there(*d))
        def _():
            pl.semaphore_signal(barrier, inc=1, device_id=device(*d))
    for name, count, me in axes:
        for step in range(1, count):
            pl.semaphore_signal(barrier, inc=1, device_id={name: (me + step) % count})

    def iota(n, dim):
        return lax.broadcasted_iota(jnp.int32, (n, 1) if dim == 0 else (1, n), dim)

    def fold(index, first, total, level):
        base = first >> level
        ok = jnp.logical_and(index + base >= 0, index + base < (total >> level))
        return jnp.where(ok, index, FAR)

    row0, col0 = row * nr, cx * nc
    r1, r2 = nr // 2 + 16, nr // 4 + 16
    c1, c2 = nc // 2 + 128, nc // 4 + 128
    r3, r4, r5, r6 = t3 + 2 * EDGE3, nr // 16 + 32, nr // 32 + 16, nr // 64 + 8

    def rows_at(level, dim):
        if level == 0:
            p = iota(nr + 2 * HALO, dim)
            return jnp.where(p < nr, p, jnp.where(p < nr + HALO, p - nr - HALO, p - HALO))
        count, shift = ((r1, 8), (r2, 8), (r3, EDGE3), (r4, 16), (r5, 8), (r6, 4))[level - 1]
        return iota(count, dim) - shift

    def cols_at(level, dim):
        if level == 0:
            p = iota(nc + 2 * SIDE, dim)
            return jnp.where(p < nc, p, jnp.where(p < nc + SIDE, p - nc - SIDE, p - SIDE))
        if level < 3:
            return iota((c1, c2)[level - 1], dim) - 8
        if level == 3:
            p = iota(6 * w3, dim)
            return (p // (2 * w3) - 1) * w3 + p % w3
        return iota(2 * w3, dim) % w3 - (16, 8, 4)[level - 4]

    def kind(count, dim):
        return (iota(count, dim) // w3) % 2

    def reduce_rows(level):
        out = fold(rows_at(level + 1, 0), row0, rows_total, level + 1)
        return band(rows_at(level, 1) - 2 * out, 1.0)

    def reduce_cols(level):
        out = fold(cols_at(level + 1, 1), col0, cols_total, level + 1)
        distance = cols_at(level, 0) - 2 * out
        if level >= 3:
            same = kind(distance.shape[0], 0) == kind(distance.shape[1], 1)
            distance = jnp.where(same, distance, FAR)
        return band(distance, 1.0)

    def expand_rows(level):
        out = iota(nr, 0) if level == 0 else rows_at(level, 0)
        return band(2 * rows_at(level + 1, 1) - out, 2.0)

    def expand_cols(level):
        out = iota(nc, 1) if level == 0 else cols_at(level, 1)
        return band(2 * cols_at(level + 1, 0) - out, 2.0)

    def lookup(masks, table):
        values = [table[i] for i in range(table.shape[0])]
        for mask in masks:
            values = [
                jnp.where(mask, values[i + 1], values[i]) for i in range(0, len(values), 2)
            ]
        return values[0]

    bits = (off_ref.shape[0] - 1).bit_length()

    def level0(rows, cols, valid):
        ids = s_buf[rows, cols]
        masks = [(ids & (1 << bit)) != 0 for bit in range(bits)]
        weight = lookup(masks, wgt_ref)
        moved = h_buf[rows, cols] + lookup(masks, off_ref)
        numer = weight * moved
        if valid is not None:
            weight = jnp.where(valid, weight, 0.0)
            numer = jnp.where(valid, numer, 0.0)
        nh[rows, cols], nl[rows, cols] = split(numer)
        dh[rows, cols], dl[rows, cols] = split(weight)
        return moved

    for copy in own:
        copy.wait()

    step = 32

    def own_rows(i, carry):
        rows = pl.ds(pl.multiple_of(i * step, step), step)
        q0[rows, :] = level0(rows, pl.ds(0, nc), None)
        return carry

    lax.fori_loop(0, nr // step, own_rows, 0)

    reduce0, cols0 = reduce_rows(0), reduce_cols(0)

    near = sum(there(*d).astype(jnp.int32) for d in dirs)
    pl.semaphore_wait(barrier, near + (nx + ny + nz - 3))

    def rim(i, a, d):
        drow, dcol = d
        src, dst = ((h_ref, h_buf), (s_ref, s_buf))[a]
        rs = {-1: (0, nr + HALO, HALO), 0: (0, 0, nr), 1: (nr - HALO, nr, HALO)}[drow]
        cs = {-1: (0, nc + SIDE, SIDE), 0: (0, 0, nc), 1: (nc - SIDE, nc, SIDE)}[dcol]
        return pltpu.make_async_remote_copy(
            src_ref=src.at[pl.ds(rs[0], rs[2]), pl.ds(cs[0], cs[2])],
            dst_ref=dst.at[pl.ds(rs[1], rs[2]), pl.ds(cs[1], cs[2])],
            send_sem=send0.at[2 * i + a],
            recv_sem=recv0.at[2 * i + a],
            device_id=device(*d),
        )

    for i, d in enumerate(dirs):
        @pl.when(there(*d))
        def _():
            for a in range(2):
                rim(i, a, d).start()

    u_high, u_low = split(u_buf[...])
    pick = iota(16, 0)
    u_rows = jnp.where(
        pick == 0, u_high.astype(F32), jnp.where(pick == 1, u_low.astype(F32), 0.0)
    ).astype(BF16)
    top = jnp.concatenate([reduce0[:, :nr], u_rows], axis=0)
    rim0 = reduce0[:, nr:]

    def dot(a, b):
        return jnp.dot(a, b, preferred_element_type=F32)

    tn = dot(top, nh[pl.ds(0, nr), pl.ds(0, nc)]) + dot(top, nl[pl.ds(0, nr), pl.ds(0, nc)])
    td = dot(top, dh[pl.ds(0, nr), pl.ds(0, nc)]) + dot(top, dl[pl.ds(0, nr), pl.ds(0, nc)])
    v_row = v_buf[...]
    sum_n = jnp.sum(tn[r1:, :] * v_row)
    sum_d = jnp.sum(td[r1:, :] * v_row)

    tile_row = lax.broadcasted_iota(jnp.int32, (8, 128), 0)
    part[0] = jnp.where(tile_row == 0, sum_n, jnp.where(tile_row == 1, sum_d, 0.0))

    starts = (0, nx - 1, nx + nz - 2)

    def phase(k):
        name, count, me = axes[k]
        return [
            pltpu.make_async_remote_copy(
                src_ref=part.at[k],
                dst_ref=slots.at[starts[k] + s - 1],
                send_sem=psend.at[starts[k] + s - 1],
                recv_sem=precv.at[starts[k] + s - 1],
                device_id={name: (me + s) % count},
            )
            for s in range(1, count)
        ]

    def finish(k):
        total = part[k]
        for s, copy in enumerate(phase(k)):
            copy.wait()
            total = total + slots[starts[k] + s]
        return total

    for copy in phase(0):
        copy.start()

    q0_copy = pltpu.make_async_copy(q0, q0_ref, own_sem.at[4])
    q0_copy.start()

    def take(ds):
        for i, d in enumerate(dirs):
            if d in ds:
                @pl.when(there(*d))
                def _():
                    for a in range(2):
                        rim(i, a, d).wait_send()

                @pl.when(there(-d[0], -d[1]))
                def _():
                    for a in range(2):
                        rim(i, a, d).wait_recv()

    def yes(flag):
        return flag.astype(jnp.int32)

    up, down = yes(row > 0), yes(row < blocks - 1)
    west, east = yes(cx > 0), yes(cx < nx - 1)
    side_ok = jnp.where(iota(2 * SIDE, 1) < SIDE, west, east)
    rim_ok = jnp.where(iota(2 * HALO, 0) < HALO, up, down)
    body, rim_r = pl.ds(0, nr), pl.ds(nr, 2 * HALO)
    middle, side_c = pl.ds(0, nc), pl.ds(nc, 2 * SIDE)

    take([d for d in dirs if d[0] == 0])

    def side_rows(i, carry):
        rows = pl.ds(pl.multiple_of(i * step, step), step)
        level0(rows, side_c, jnp.broadcast_to(side_ok, (step, 2 * SIDE)) > 0)
        return carry

    lax.fori_loop(0, nr // step, side_rows, 0)

    def level1(t_own, high, low):
        t_side = dot(reduce0[:, :nr], high[body, side_c]) + dot(reduce0[:, :nr], low[body, side_c])
        return right(t_own[:r1, :], cols0[:nc]) + right(t_side, cols0[nc:])

    n1, d1 = level1(tn, nh, nl), level1(td, dh, dl)

    part[1] = finish(0)
    for copy in phase(1):
        copy.start()

    rows1, cols1 = reduce_rows(1), reduce_cols(1)
    n2, d2 = left(rows1, right(n1, cols1)), left(rows1, right(d1, cols1))

    own_out = iota(2 * w3, 1)
    in2 = cols_at(2, 0)
    pick_n = band(jnp.where(own_out < w3, in2 - 2 * own_out, FAR), 1.0)
    pick_d = band(jnp.where(own_out < w3, FAR, in2 - 2 * (own_out - w3)), 1.0)
    own_rows3 = band(rows_at(2, 1) - 2 * iota(t3, 0), 1.0)
    both = left(own_rows3, right(n2, pick_n) + right(d2, pick_d))

    def ends(count):
        p = iota(32, 0)
        return jnp.where(p < 16, p, count - 32 + p)

    def ends_in(count):
        p = iota(32, 1)
        return jnp.where(p < 16, p, count - 32 + p)

    ends0 = band(
        (iota(2 * HALO, 1) + jnp.where(iota(2 * HALO, 1) < HALO, -HALO, nr - HALO))
        - 2 * fold(ends(r1) - 8, row0, rows_total, 1), 1.0,
    )
    ends1 = band((ends_in(r1) - 8) - 2 * fold(ends(r2) - 8, row0, rows_total, 2), 1.0)
    ends2 = band((ends_in(r2) - 8) - 2 * ends(t3), 1.0)

    def patch(x, e):
        n = x.shape[0]
        return jnp.concatenate([x[:16] + e[:16], x[16 : n - 16], x[n - 16 :] + e[16:]], axis=0)

    take([d for d in dirs if d[0] != 0])
    level0(rim_r, middle, jnp.broadcast_to(rim_ok, (2 * HALO, nc)) > 0)
    level0(rim_r, side_c, jnp.broadcast_to(rim_ok * side_ok, (2 * HALO, 2 * SIDE)) > 0)

    def pair(x):
        return x[:32], x[32:]

    stacked = dot(jnp.concatenate([nh[rim_r, :], dh[rim_r, :]], axis=0), cols0) + dot(
        jnp.concatenate([nl[rim_r, :], dl[rim_r, :]], axis=0), cols0
    )
    e1 = [left(ends0, x) for x in pair(stacked)]
    e2 = [left(ends1, x) for x in pair(right(jnp.concatenate(e1, axis=0), cols1))]
    e3 = left(ends2, right(e2[0], pick_n) + right(e2[1], pick_d))
    b3[1, pl.ds(EDGE3, t3), :] = patch(both, e3)

    def rim3(i, d):
        drow, dcol = d
        rs = {
            -1: (EDGE3, EDGE3 + t3, EDGE3),
            0: (EDGE3, EDGE3, t3),
            1: (t3, 0, EDGE3),
        }[drow]
        return pltpu.make_async_remote_copy(
            src_ref=b3.at[1, pl.ds(rs[0], rs[2]), :],
            dst_ref=b3.at[1 - dcol, pl.ds(rs[1], rs[2]), :],
            send_sem=send3.at[i],
            recv_sem=recv3.at[i],
            device_id=device(*d),
        )

    for i, d in enumerate(dirs):
        @pl.when(there(*d))
        def _():
            rim3(i, d).start()

    n1, d1, n2, d2 = patch(n1, e1[0]), patch(d1, e1[1]), patch(n2, e2[0]), patch(d2, e2[1])
    q1 = jnp.where(d1 > 0, n1 / d1, 0.0)
    q2 = jnp.where(d2 > 0, n2 / d2, 0.0)
    part[2] = finish(1)
    for copy in phase(2):
        copy.start()

    rows_ = [None, None, None] + [reduce_rows(level) for level in (3, 4, 5)]
    cols_ = [None, None, None] + [reduce_cols(level) for level in (3, 4, 5)]
    up_rows = [None] + [expand_rows(level) for level in range(1, 6)]
    up_cols = [None] + [expand_cols(level) for level in range(1, 6)]

    for i, d in enumerate(dirs):
        @pl.when(there(*d))
        def _():
            rim3(i, d).wait_send()

        @pl.when(there(-d[0], -d[1]))
        def _():
            rim3(i, d).wait_recv()

    p3 = iota(r3, 0)
    ok3 = jnp.where(p3 < EDGE3, up, jnp.where(p3 < EDGE3 + t3, 1, down))
    lane = iota(2 * w3, 1)

    def ratio(packed):
        weights = pltpu.roll(packed, w3, axis=1)
        ok = jnp.logical_and(weights > 0, jnp.broadcast_to(lane, packed.shape) < w3)
        return jnp.where(ok, packed / weights, 0.0), ok

    pieces = []
    for block, flag in ((0, west), (1, None), (2, east)):
        ok = ok3 if flag is None else ok3 * flag
        piece = b3[block]
        pieces.append(jnp.where(jnp.broadcast_to(ok, piece.shape) > 0, piece, 0.0))
    packed = jnp.concatenate(pieces, axis=1)
    q3 = [ratio(piece) for piece in pieces]
    q3, ok_3 = [q for q, _ in q3], [jnp.where(ok, 1.0, 0.0) for _, ok in q3]
    q3, ok_3 = jnp.concatenate(q3, axis=1), jnp.concatenate(ok_3, axis=1) > 0

    v4 = left(rows_[3], right(packed, cols_[3]))
    v5 = left(rows_[4], right(v4, cols_[4]))
    v6 = left(rows_[5], right(v5, cols_[5]))
    q4, ok_4 = ratio(v4)
    q5, ok_5 = ratio(v5)
    q6, ok_6 = ratio(v6)

    total = finish(2)
    top_sum = jnp.sum(jnp.where(tile_row == 0, total, 0.0), axis=0, keepdims=True)
    top_weight = jnp.sum(jnp.where(tile_row == 1, total, 0.0), axis=0, keepdims=True)
    top_mean = (top_sum / top_weight)[:, :1]

    z = jnp.where(ok_6, top_mean - gain_ref[5] * q6, 0.0)
    levels = ((5, q5, ok_5), (4, q4, ok_4), (3, q3, ok_3), (2, q2, d2 > 0), (1, q1, d1 > 0))
    for level, q, ok in levels:
        grown = left(up_rows[level], right(z, up_cols[level]))
        z = jnp.where(ok, grown + (gain_ref[level] - gain_ref[level - 1]) * q, 0.0)
    z1_ref[...] = z
    q0_copy.wait()


def last(gain_ref, z_ref, q_hbm, out_ref, q_buf, sem):
    nr, nc = out_ref.shape
    block = nr // 4
    copies = [
        pltpu.make_async_copy(
            q_hbm.at[pl.ds(i * block, block), :], q_buf.at[pl.ds(i * block, block), :], sem.at[i]
        )
        for i in range(4)
    ]
    for copy in copies:
        copy.start()
    tall = block // 2 + 16

    def iota(n, dim):
        return lax.broadcasted_iota(jnp.int32, (n, 1) if dim == 0 else (1, n), dim)

    cols = band(2 * (iota(z_ref.shape[1], 0) - 8) - iota(nc, 1), 2.0)
    rows = band(2 * (iota(tall, 1) - 8) - iota(block, 0), 2.0)
    gain = gain_ref[0]
    wide = right(z_ref[...], cols)
    for i in range(4):
        grown = left(rows, wide[i * block // 2 : i * block // 2 + tall])
        copies[i].wait()
        here = pl.ds(i * block, block)
        out_ref[here, :] = gain * q_buf[here, :] + grown


def local(mesh_shape, heights, scene_ids, scene_offset, scene_weight, band_gain):
    nx, ny, nz = mesh_shape
    nr, nc = heights.shape
    rows_total, cols_total = nr * ny * nz, nc * nx
    u = jnp.asarray(reach(rows_total).reshape(ny * nz, 1, nr))
    v = jnp.asarray(reach(cols_total).reshape(nx, 1, nc))
    sizes = (nr, nc, nx, ny, nz, rows_total, cols_total)
    ext = (nr + 2 * HALO, nc + 2 * SIDE)
    peers = nx + ny + nz - 3
    smem = pl.BlockSpec(memory_space=pltpu.SMEM)
    hbm = pl.BlockSpec(memory_space=pl.ANY)
    z1, q0 = pl.pallas_call(
        functools.partial(kernel, sizes),
        out_shape=(
            jax.ShapeDtypeStruct((nr // 2 + 16, nc // 2 + 128), F32),
            jax.ShapeDtypeStruct((nr, nc), F32),
        ),
        in_specs=[smem, smem, smem, hbm, hbm, hbm, hbm],
        out_specs=(pl.BlockSpec(memory_space=pltpu.VMEM), hbm),
        scratch_shapes=[
            pltpu.VMEM((nr, nc), F32),
            pltpu.VMEM(ext, F32),
            pltpu.VMEM(ext, jnp.int32),
            pltpu.VMEM((1, nr), F32),
            pltpu.VMEM((1, nc), F32),
            pltpu.VMEM(ext, BF16),
            pltpu.VMEM(ext, BF16),
            pltpu.VMEM(ext, BF16),
            pltpu.VMEM(ext, BF16),
            pltpu.VMEM((3, nr // 8 + 2 * EDGE3, nc // 4), F32),
            pltpu.VMEM((3, 8, 128), F32),
            pltpu.VMEM((peers, 8, 128), F32),
            pltpu.SemaphoreType.DMA((5,)),
            pltpu.SemaphoreType.DMA((16,)),
            pltpu.SemaphoreType.DMA((16,)),
            pltpu.SemaphoreType.DMA((8,)),
            pltpu.SemaphoreType.DMA((8,)),
            pltpu.SemaphoreType.DMA((peers,)),
            pltpu.SemaphoreType.DMA((peers,)),
        ],
        compiler_params=pltpu.CompilerParams(collective_id=0, has_side_effects=True),
    )(scene_offset, scene_weight, band_gain, heights, scene_ids, u, v)
    vmem = pl.BlockSpec(memory_space=pltpu.VMEM)
    return pl.pallas_call(
        last,
        out_shape=jax.ShapeDtypeStruct((nr, nc), F32),
        in_specs=[smem, vmem, hbm],
        out_specs=vmem,
        scratch_shapes=[pltpu.VMEM((nr, nc), F32), pltpu.SemaphoreType.DMA((4,))],
    )(band_gain, z1, q0)


def solution(mesh):
    placed = (P(("gy", "gz"), "gx"), P(("gy", "gz"), "gx"), P(), P(), P())
    shape = tuple(mesh.shape[name] for name in ("gx", "gy", "gz"))
    return jax.shard_map(
        functools.partial(local, shape), mesh=mesh, in_specs=placed,
        out_specs=P(("gy", "gz"), "gx"), check_vma=False,
    )
```

```python
import functools

import jax
import jax.numpy as jnp
import numpy as np
from jax import lax
from jax.experimental import pallas as pl
from jax.experimental.pallas import tpu as pltpu
from jax.sharding import PartitionSpec as P

F32, BF16 = jnp.float32, jnp.bfloat16
FAR = 1 << 20
HALO = 16
SIDE = 128
EDGE3 = 24
TAPS = (0.375, 0.25, 0.0625)
LEVELS = 6


def reach(count):
    weights = np.ones(count >> LEVELS, np.float64)
    for _ in range(LEVELS):
        fine = np.zeros(2 * weights.size + 4, np.float64)
        for tap, value in zip(range(-2, 3), (0.0625, 0.25, 0.375, 0.25, 0.0625)):
            fine[2 + tap : 2 + tap + 2 * weights.size : 2] += value * weights
        weights = fine[2:-2]
    return weights.astype(np.float32)


def split(x):
    high = x.astype(BF16)
    return high, (x - high.astype(F32)).astype(BF16)


def right(x, c):
    high, low = split(x)
    return jnp.dot(high, c, preferred_element_type=F32) + jnp.dot(
        low, c, preferred_element_type=F32
    )


def left(r, x):
    high, low = split(x)
    return jnp.dot(r, high, preferred_element_type=F32) + jnp.dot(
        r, low, preferred_element_type=F32
    )


def band(distance, scale):
    far = jnp.abs(distance)
    value = jnp.where(far == 2, TAPS[2] * scale, 0.0)
    value = jnp.where(far == 1, TAPS[1] * scale, value)
    value = jnp.where(far == 0, TAPS[0] * scale, value)
    return value.astype(F32).astype(BF16)


def kernel(
    sizes, off_ref, wgt_ref, gain_ref, h_ref, s_ref, u_ref, v_ref, z1_ref, q0_ref,
    q0, h_buf, s_buf, u_buf, v_buf, nh, nl, dh, dl, b3, part, slots,
    own_sem, send0, recv0, send3, recv3, psend, precv,
):
    nr, nc, nx, ny, nz, rows_total, cols_total = sizes
    cx, cy, cz = lax.axis_index("gx"), lax.axis_index("gy"), lax.axis_index("gz")
    row = cy * nz + cz
    blocks = ny * nz
    w3 = nc // 8
    t3 = nr // 8

    def device(drow, dcol):
        target = row + drow
        return {"gx": cx + dcol, "gy": target // nz, "gz": target % nz}

    has = {-1: (row > 0, cx > 0), 0: None, 1: (row < blocks - 1, cx < nx - 1)}

    def there(drow, dcol):
        ok = None
        if drow:
            ok = has[drow][0]
        if dcol:
            ok = has[dcol][1] if ok is None else jnp.logical_and(ok, has[dcol][1])
        return ok

    dirs = [(a, b) for a in (-1, 0, 1) for b in (-1, 0, 1) if a or b]
    axes = (("gx", nx, cx), ("gz", nz, cz), ("gy", ny, cy))

    own = []
    for i, (src, dst) in enumerate(
        (
            (h_ref, h_buf.at[pl.ds(0, nr), pl.ds(0, nc)]),
            (s_ref, s_buf.at[pl.ds(0, nr), pl.ds(0, nc)]),
            (u_ref.at[row], u_buf),
            (v_ref.at[cx], v_buf),
        )
    ):
        copy = pltpu.make_async_copy(src, dst, own_sem.at[i])
        copy.start()
        own.append(copy)

    barrier = pltpu.get_barrier_semaphore()
    for d in dirs:
        @pl.when(there(*d))
        def _():
            pl.semaphore_signal(barrier, inc=1, device_id=device(*d))
    for name, count, me in axes:
        for step in range(1, count):
            pl.semaphore_signal(barrier, inc=1, device_id={name: (me + step) % count})

    def iota(n, dim):
        return lax.broadcasted_iota(jnp.int32, (n, 1) if dim == 0 else (1, n), dim)

    def fold(index, first, total, level):
        base = first >> level
        ok = jnp.logical_and(index + base >= 0, index + base < (total >> level))
        return jnp.where(ok, index, FAR)

    row0, col0 = row * nr, cx * nc
    r1, r2 = nr // 2 + 16, nr // 4 + 16
    c1, c2 = nc // 2 + 128, nc // 4 + 128
    r3, r4, r5, r6 = t3 + 2 * EDGE3, nr // 16 + 32, nr // 32 + 16, nr // 64 + 8

    def rows_at(level, dim):
        if level == 0:
            p = iota(nr + 2 * HALO, dim)
            return jnp.where(p < nr, p, jnp.where(p < nr + HALO, p - nr - HALO, p - HALO))
        count, shift = ((r1, 8), (r2, 8), (r3, EDGE3), (r4, 16), (r5, 8), (r6, 4))[level - 1]
        return iota(count, dim) - shift

    def cols_at(level, dim):
        if level == 0:
            p = iota(nc + 2 * SIDE, dim)
            return jnp.where(p < nc, p, jnp.where(p < nc + SIDE, p - nc - SIDE, p - SIDE))
        if level < 3:
            return iota((c1, c2)[level - 1], dim) - 8
        if level == 3:
            p = iota(6 * w3, dim)
            return (p // (2 * w3) - 1) * w3 + p % w3
        return iota(2 * w3, dim) % w3 - (16, 8, 4)[level - 4]

    def kind(count, dim):
        return (iota(count, dim) // w3) % 2

    def reduce_rows(level):
        out = fold(rows_at(level + 1, 0), row0, rows_total, level + 1)
        return band(rows_at(level, 1) - 2 * out, 1.0)

    def reduce_cols(level):
        out = fold(cols_at(level + 1, 1), col0, cols_total, level + 1)
        distance = cols_at(level, 0) - 2 * out
        if level >= 3:
            same = kind(distance.shape[0], 0) == kind(distance.shape[1], 1)
            distance = jnp.where(same, distance, FAR)
        return band(distance, 1.0)

    def expand_rows(level):
        out = iota(nr, 0) if level == 0 else rows_at(level, 0)
        return band(2 * rows_at(level + 1, 1) - out, 2.0)

    def expand_cols(level):
        out = iota(nc, 1) if level == 0 else cols_at(level, 1)
        return band(2 * cols_at(level + 1, 0) - out, 2.0)

    def lookup(masks, table):
        values = [table[i] for i in range(table.shape[0])]
        for mask in masks:
            values = [
                jnp.where(mask, values[i + 1], values[i]) for i in range(0, len(values), 2)
            ]
        return values[0]

    bits = (off_ref.shape[0] - 1).bit_length()

    def level0(rows, cols, valid):
        ids = s_buf[rows, cols]
        masks = [(ids & (1 << bit)) != 0 for bit in range(bits)]
        weight = lookup(masks, wgt_ref)
        moved = h_buf[rows, cols] + lookup(masks, off_ref)
        numer = weight * moved
        if valid is not None:
            weight = jnp.where(valid, weight, 0.0)
            numer = jnp.where(valid, numer, 0.0)
        nh[rows, cols], nl[rows, cols] = split(numer)
        dh[rows, cols], dl[rows, cols] = split(weight)
        return moved

    for copy in own:
        copy.wait()

    step = 32

    def own_rows(i, carry):
        rows = pl.ds(pl.multiple_of(i * step, step), step)
        q0[rows, :] = level0(rows, pl.ds(0, nc), None)
        return carry

    lax.fori_loop(0, nr // step, own_rows, 0)

    near = sum(there(*d).astype(jnp.int32) for d in dirs)
    pl.semaphore_wait(barrier, near + (nx + ny + nz - 3))

    def rim(i, a, d):
        drow, dcol = d
        src, dst = ((h_ref, h_buf), (s_ref, s_buf))[a]
        rs = {-1: (0, nr + HALO, HALO), 0: (0, 0, nr), 1: (nr - HALO, nr, HALO)}[drow]
        cs = {-1: (0, nc + SIDE, SIDE), 0: (0, 0, nc), 1: (nc - SIDE, nc, SIDE)}[dcol]
        return pltpu.make_async_remote_copy(
            src_ref=src.at[pl.ds(rs[0], rs[2]), pl.ds(cs[0], cs[2])],
            dst_ref=dst.at[pl.ds(rs[1], rs[2]), pl.ds(cs[1], cs[2])],
            send_sem=send0.at[2 * i + a],
            recv_sem=recv0.at[2 * i + a],
            device_id=device(*d),
        )

    for i, d in enumerate(dirs):
        @pl.when(there(*d))
        def _():
            for a in range(2):
                rim(i, a, d).start()

    def dot(a, b):
        return jnp.dot(a, b, preferred_element_type=F32)

    own_out = iota(2 * w3, 1)
    in2 = cols_at(2, 0)
    pick_n = band(jnp.where(own_out < w3, in2 - 2 * own_out, FAR), 1.0)
    pick_d = band(jnp.where(own_out < w3, FAR, in2 - 2 * (own_out - w3)), 1.0)
    own_rows3 = band(rows_at(2, 1) - 2 * iota(t3, 0), 1.0)
    reduce0, rows1 = reduce_rows(0), reduce_rows(1)
    rows03 = dot(dot(own_rows3, rows1).astype(BF16), reduce0)
    rows03 = jnp.concatenate(split(rows03), axis=0)
    u_high, u_low = split(u_buf[...])
    pick = iota(16, 0)
    u_rows = jnp.where(
        pick == 0, u_high.astype(F32), jnp.where(pick == 1, u_low.astype(F32), 0.0)
    ).astype(BF16)
    top = jnp.concatenate([rows03[:, :nr], u_rows], axis=0)

    def own_part(high, low):
        rows, cols = pl.ds(0, nr), pl.ds(0, nc)
        return dot(top, high[rows, cols]) + dot(top, low[rows, cols])

    tn, td = own_part(nh, nl), own_part(dh, dl)
    v_row = v_buf[...]
    sum_n = jnp.sum(tn[2 * t3 :, :] * v_row)
    sum_d = jnp.sum(td[2 * t3 :, :] * v_row)

    tile_row = lax.broadcasted_iota(jnp.int32, (8, 128), 0)
    part[0] = jnp.where(tile_row == 0, sum_n, jnp.where(tile_row == 1, sum_d, 0.0))

    starts = (0, nx - 1, nx + nz - 2)

    def phase(k):
        name, count, me = axes[k]
        return [
            pltpu.make_async_remote_copy(
                src_ref=part.at[k],
                dst_ref=slots.at[starts[k] + s - 1],
                send_sem=psend.at[starts[k] + s - 1],
                recv_sem=precv.at[starts[k] + s - 1],
                device_id={name: (me + s) % count},
            )
            for s in range(1, count)
        ]

    def finish(k):
        total = part[k]
        for s, copy in enumerate(phase(k)):
            copy.wait()
            total = total + slots[starts[k] + s]
        return total

    for copy in phase(0):
        copy.start()

    q0_copy = pltpu.make_async_copy(q0, q0_ref, own_sem.at[4])
    q0_copy.start()

    def take(ds):
        for i, d in enumerate(dirs):
            if d in ds:
                @pl.when(there(*d))
                def _():
                    for a in range(2):
                        rim(i, a, d).wait_send()

                @pl.when(there(-d[0], -d[1]))
                def _():
                    for a in range(2):
                        rim(i, a, d).wait_recv()

    def yes(flag):
        return flag.astype(jnp.int32)

    up, down = yes(row > 0), yes(row < blocks - 1)
    west, east = yes(cx > 0), yes(cx < nx - 1)
    side_ok = jnp.where(iota(2 * SIDE, 1) < SIDE, west, east)
    rim_ok = jnp.where(iota(2 * HALO, 0) < HALO, up, down)
    body, rim_r = pl.ds(0, nr), pl.ds(nr, 2 * HALO)
    middle, side_c = pl.ds(0, nc), pl.ds(nc, 2 * SIDE)

    take([d for d in dirs if d[0] == 0])

    def side_rows(i, carry):
        rows = pl.ds(pl.multiple_of(i * step, step), step)
        level0(rows, side_c, jnp.broadcast_to(side_ok, (step, 2 * SIDE)) > 0)
        return carry

    lax.fori_loop(0, nr // step, side_rows, 0)

    cols0, cols1 = reduce_cols(0), reduce_cols(1)
    cols02 = dot(cols0, cols1).astype(BF16)
    cols03 = [split(dot(cols02, pick)) for pick in (pick_n, pick_d)]

    def side_part(t, high, low):
        t_side = dot(rows03[:, :nr], high[body, side_c]) + dot(rows03[:, :nr], low[body, side_c])
        t = jnp.concatenate([t[: 2 * t3], t_side], axis=1)
        return t[:t3] + t[t3:]

    tn, td = side_part(tn, nh, nl), side_part(td, dh, dl)

    part[1] = finish(0)
    for copy in phase(1):
        copy.start()

    half, start = nr // 4, nr // 2 - 32
    reduce0_b = band(
        start + iota(nr - start, 1) - 2 * fold(iota(r1 - half, 0) + (half - 8), row0, rows_total, 1), 1.0
    )

    def level1(x):
        t = [dot(reduce0[:half, : nr // 2], part_[pl.ds(0, nr // 2), :]) for part_ in x]
        b = [dot(reduce0_b, part_[pl.ds(start, nr - start), :]) for part_ in x]
        t = jnp.concatenate([t[0] + t[1], b[0] + b[1]], axis=0)
        low, high = split(t)

        def wide(k0, k1, n0, n1):
            return dot(low[:, k0:k1], cols0[k0:k1, n0:n1]) + dot(high[:, k0:k1], cols0[k0:k1, n0:n1])

        edge = nc // 2
        return jnp.concatenate(
            [
                wide(0, nc + SIDE, 0, edge),
                wide(nc - SIDE, nc, edge, c1) + wide(nc + SIDE, nc + 2 * SIDE, edge, c1),
            ],
            axis=1,
        )

    n1, d1 = level1((nh, nl)), level1((dh, dl))

    take([d for d in dirs if d[0] != 0])
    level0(rim_r, middle, jnp.broadcast_to(rim_ok, (2 * HALO, nc)) > 0)
    level0(rim_r, side_c, jnp.broadcast_to(rim_ok * side_ok, (2 * HALO, 2 * SIDE)) > 0)

    def rim_part(t, high, low, cols):
        e = dot(rows03[:, nr:], high[rim_r, :]) + dot(rows03[:, nr:], low[rim_r, :])
        t = t + e[:t3] + e[t3:]
        t_high, t_low = split(t)
        return dot(t_high, cols[0]) + dot(t_low, cols[0]) + dot(t_high, cols[1])

    b3[1, pl.ds(EDGE3, t3), :] = rim_part(tn, nh, nl, cols03[0]) + rim_part(td, dh, dl, cols03[1])

    def rim3(i, d):
        drow, dcol = d
        rs = {
            -1: (EDGE3, EDGE3 + t3, EDGE3),
            0: (EDGE3, EDGE3, t3),
            1: (t3, 0, EDGE3),
        }[drow]
        return pltpu.make_async_remote_copy(
            src_ref=b3.at[1, pl.ds(rs[0], rs[2]), :],
            dst_ref=b3.at[1 - dcol, pl.ds(rs[1], rs[2]), :],
            send_sem=send3.at[i],
            recv_sem=recv3.at[i],
            device_id=device(*d),
        )

    for i, d in enumerate(dirs):
        @pl.when(there(*d))
        def _():
            rim3(i, d).start()

    def ends(count):
        p = iota(32, 0)
        return jnp.where(p < 16, p, count - 32 + p)

    rim_in = iota(2 * HALO, 1)
    rim_in = rim_in + jnp.where(rim_in < HALO, -HALO, nr - HALO)
    ends0 = band(rim_in - 2 * fold(ends(r1) - 8, row0, rows_total, 1), 1.0)

    def patch(x, high, low):
        e = left(ends0, dot(high[rim_r, :], cols0) + dot(low[rim_r, :], cols0))
        n = x.shape[0]
        return jnp.concatenate([x[:16] + e[:16], x[16 : n - 16], x[n - 16 :] + e[16:]], axis=0)

    n1, d1 = patch(n1, nh, nl), patch(d1, dh, dl)
    part[2] = finish(1)
    for copy in phase(2):
        copy.start()
    q1 = jnp.where(d1 > 0, n1 / d1, 0.0)
    n2, d2 = left(rows1, right(n1, cols1)), left(rows1, right(d1, cols1))
    q2 = jnp.where(d2 > 0, n2 / d2, 0.0)

    rows_ = [None, None, None] + [reduce_rows(level) for level in (3, 4, 5)]
    cols_ = [None, None, None] + [reduce_cols(level) for level in (3, 4, 5)]
    up_rows = [None] + [expand_rows(level) for level in range(1, 6)]
    up_cols = [None] + [expand_cols(level) for level in range(1, 6)]

    for i, d in enumerate(dirs):
        @pl.when(there(*d))
        def _():
            rim3(i, d).wait_send()

        @pl.when(there(-d[0], -d[1]))
        def _():
            rim3(i, d).wait_recv()

    p3 = iota(r3, 0)
    ok3 = jnp.where(p3 < EDGE3, up, jnp.where(p3 < EDGE3 + t3, 1, down))
    lane = iota(2 * w3, 1)

    def ratio(packed):
        weights = pltpu.roll(packed, w3, axis=1)
        ok = jnp.logical_and(weights > 0, jnp.broadcast_to(lane, packed.shape) < w3)
        return jnp.where(ok, packed / weights, 0.0), ok

    pieces = []
    for block, flag in ((0, west), (1, None), (2, east)):
        ok = ok3 if flag is None else ok3 * flag
        piece = b3[block]
        pieces.append(jnp.where(jnp.broadcast_to(ok, piece.shape) > 0, piece, 0.0))
    packed = jnp.concatenate(pieces, axis=1)
    q3 = [ratio(piece) for piece in pieces]
    q3, ok_3 = [q for q, _ in q3], [jnp.where(ok, 1.0, 0.0) for _, ok in q3]
    q3, ok_3 = jnp.concatenate(q3, axis=1), jnp.concatenate(ok_3, axis=1) > 0

    v4 = left(rows_[3], right(packed, cols_[3]))
    v5 = left(rows_[4], right(v4, cols_[4]))
    v6 = left(rows_[5], right(v5, cols_[5]))
    q4, ok_4 = ratio(v4)
    q5, ok_5 = ratio(v5)
    q6, ok_6 = ratio(v6)

    total = finish(2)
    top_sum = jnp.sum(jnp.where(tile_row == 0, total, 0.0), axis=0, keepdims=True)
    top_weight = jnp.sum(jnp.where(tile_row == 1, total, 0.0), axis=0, keepdims=True)
    top_mean = (top_sum / top_weight)[:, :1]

    z = jnp.where(ok_6, top_mean - gain_ref[5] * q6, 0.0)
    levels = ((5, q5, ok_5), (4, q4, ok_4), (3, q3, ok_3), (2, q2, d2 > 0), (1, q1, d1 > 0))
    for level, q, ok in levels:
        grown = left(up_rows[level], right(z, up_cols[level]))
        z = jnp.where(ok, grown + (gain_ref[level] - gain_ref[level - 1]) * q, 0.0)
    z1_ref[...] = z
    q0_copy.wait()


def last(gain_ref, z_ref, q_hbm, out_ref, q_buf, out_buf, sem):
    nr, nc = out_buf.shape
    block = nr // 4
    copies = [
        pltpu.make_async_copy(
            q_hbm.at[pl.ds(i * block, block), :], q_buf.at[pl.ds(i * block, block), :], sem.at[i]
        )
        for i in range(4)
    ]
    for copy in copies:
        copy.start()
    tall = block // 2 + 16

    def iota(n, dim):
        return lax.broadcasted_iota(jnp.int32, (n, 1) if dim == 0 else (1, n), dim)

    cols = band(2 * (iota(z_ref.shape[1], 0) - 8) - iota(nc, 1), 2.0)
    rows = band(2 * (iota(tall, 1) - 8) - iota(block, 0), 2.0)
    gain = gain_ref[0]
    wide = right(z_ref[...], cols)
    writes = []
    for i in range(4):
        grown = left(rows, wide[i * block // 2 : i * block // 2 + tall])
        copies[i].wait()
        here = pl.ds(i * block, block)
        out_buf[here, :] = gain * q_buf[here, :] + grown
        writes.append(pltpu.make_async_copy(out_buf.at[here, :], out_ref.at[here, :], sem.at[4 + i]))
        writes[-1].start()
    for write in writes:
        write.wait()


def local(mesh_shape, heights, scene_ids, scene_offset, scene_weight, band_gain):
    nx, ny, nz = mesh_shape
    nr, nc = heights.shape
    rows_total, cols_total = nr * ny * nz, nc * nx
    u = jnp.asarray(reach(rows_total).reshape(ny * nz, 1, nr))
    v = jnp.asarray(reach(cols_total).reshape(nx, 1, nc))
    sizes = (nr, nc, nx, ny, nz, rows_total, cols_total)
    ext = (nr + 2 * HALO, nc + 2 * SIDE)
    peers = nx + ny + nz - 3
    smem = pl.BlockSpec(memory_space=pltpu.SMEM)
    hbm = pl.BlockSpec(memory_space=pl.ANY)
    z1, q0 = pl.pallas_call(
        functools.partial(kernel, sizes),
        out_shape=(
            jax.ShapeDtypeStruct((nr // 2 + 16, nc // 2 + 128), F32),
            jax.ShapeDtypeStruct((nr, nc), F32),
        ),
        in_specs=[smem, smem, smem, hbm, hbm, hbm, hbm],
        out_specs=(pl.BlockSpec(memory_space=pltpu.VMEM), hbm),
        scratch_shapes=[
            pltpu.VMEM((nr, nc), F32),
            pltpu.VMEM(ext, F32),
            pltpu.VMEM(ext, jnp.int32),
            pltpu.VMEM((1, nr), F32),
            pltpu.VMEM((1, nc), F32),
            pltpu.VMEM(ext, BF16),
            pltpu.VMEM(ext, BF16),
            pltpu.VMEM(ext, BF16),
            pltpu.VMEM(ext, BF16),
            pltpu.VMEM((3, nr // 8 + 2 * EDGE3, nc // 4), F32),
            pltpu.VMEM((3, 8, 128), F32),
            pltpu.VMEM((peers, 8, 128), F32),
            pltpu.SemaphoreType.DMA((5,)),
            pltpu.SemaphoreType.DMA((16,)),
            pltpu.SemaphoreType.DMA((16,)),
            pltpu.SemaphoreType.DMA((8,)),
            pltpu.SemaphoreType.DMA((8,)),
            pltpu.SemaphoreType.DMA((peers,)),
            pltpu.SemaphoreType.DMA((peers,)),
        ],
        compiler_params=pltpu.CompilerParams(collective_id=0, has_side_effects=True),
    )(scene_offset, scene_weight, band_gain, heights, scene_ids, u, v)
    vmem = pl.BlockSpec(memory_space=pltpu.VMEM)
    return pl.pallas_call(
        last,
        out_shape=jax.ShapeDtypeStruct((nr, nc), F32),
        in_specs=[smem, vmem, hbm],
        out_specs=hbm,
        scratch_shapes=[
            pltpu.VMEM((nr, nc), F32),
            pltpu.VMEM((nr, nc), F32),
            pltpu.SemaphoreType.DMA((8,)),
        ],
    )(band_gain, z1, q0)


def solution(mesh):
    placed = (P(("gy", "gz"), "gx"), P(("gy", "gz"), "gx"), P(), P(), P())
    shape = tuple(mesh.shape[name] for name in ("gx", "gy", "gz"))
    return jax.shard_map(
        functools.partial(local, shape), mesh=mesh, in_specs=placed,
        out_specs=P(("gy", "gz"), "gx"), check_vma=False,
    )
```
